256 devices in a mesh: tx: 8 (over x, y_hi), ty: 32 (over y_lo, z, core).
Axes of the slice: x: 4, y: 4 (y_hi: 2, y_lo: 2; y = y_hi * 2 + y_lo), z: 8, core: 2. Of those that a mesh axis runs over, the one named last changes fastest.
Arguments:
- features: bfloat16 [1536, 32, 512], P(('tx', 'ty')), may hold values from -6 to 6
- occupancy: int32 [1536, 512], P(('tx', 'ty')), may hold values from 0 to 1, as said below
- neighbours: int32 [1536, 6], P(('tx', 'ty')), may hold values from -1 to 1535, as said below
- w_first: bfloat16 [32, 864], replicated, may hold values from -0.21875 to 0.21875
- w_second: bfloat16 [32, 864], replicated, may hold values from -0.21875 to 0.21875
- cotangent: bfloat16 [1536, 32, 512], P(('tx', 'ty')), may hold values from -6 to 6
Outputs:
- result: bfloat16 [1536, 32, 512], P(('tx', 'ty'))
- grad_features: bfloat16 [1536, 32, 512], P(('tx', 'ty'))
- grad_first: float32 [32, 864], replicated
- grad_second: float32 [32, 864], replicated
The draws below stay inside these ranges and needn't reach their ends.
Inputs may be any that keep to these rules, and one draw needn't show every extreme that they name: Bricks lie on a lattice of 16 x 96 x 1 positions; the tile of device (tx, ty) (brick rows of index tx * 32 + ty) holds positions with x in [tx * 2, (tx+1) * 2) and y in [ty * 3, (ty+1) * 3), one slot each in a drawn order. An id is device * 6 + slot. A neighbour across faces 0 and 1 lies on the same device or on the device one step lower or higher along tx with the same ty; across faces 2 and 3 on the same device or one step along ty; across faces 4 and 5 on the same device. If neighbours[s, f] = t then neighbours[t, f^1] = s. Inactive bricks have all entries -1 and no occupied voxels. `occupancy`: only active bricks have occupied voxels.
All inputs are finite; a program needn't handle non-finite values.
Results may differ from the reference program's by a relative error of at most 0.03.
The reference program's roundings to bfloat16 on the way count: a program that leaves them out, or rounds other values in their place, can miss the bound.
Values may be sent and summed in bfloat16 or wider, within the bound.
No kernel may reach another device: no remote copies, remote signals or barrier semaphores. Data moves between devices by JAX's collectives and lax.ppermute only.
A program may use at most 128 MiB of HBM per device.

```python
import math
import jax
import jax.numpy as jnp
from jax import lax

C = 32
EDGE = 8
BX = 2
BY = 3
BZ = 1
VOX = 512
SLOTS = 6
BRICKS = 1536
GRID_X = 16
GRID_Y = 96


def lattice(key):
    tiles_x = GRID_X // BX
    tiles_y = GRID_Y // BY
    level = jax.random.randint(jax.random.fold_in(key, 11), (tiles_x, tiles_y), 3, 9)
    level = level.at[tiles_x - 1, tiles_y - 1].set(8)
    tile_level = jnp.repeat(jnp.repeat(level, BX, axis=0), BY, axis=1)[:, :, None]
    dice = jax.random.randint(jax.random.fold_in(key, 12), (GRID_X, GRID_Y, BZ), 0, 8)
    active = dice < tile_level
    keys = jax.random.split(jax.random.fold_in(key, 13), tiles_x * tiles_y)
    slot_of = jax.vmap(lambda k: jax.random.permutation(k, SLOTS))(keys).astype(jnp.int32)
    pos_of = jnp.argsort(slot_of, axis=1).astype(jnp.int32)
    device = jnp.arange(tiles_x * tiles_y, dtype=jnp.int32)[:, None]
    tile_row = device // tiles_y
    tile_col = device % tiles_y
    gx = tile_row * BX + pos_of // (BY * BZ)
    gy = tile_col * BY + pos_of // BZ % BY
    gz = pos_of % BZ
    alive = active[gx, gy, gz]
    offsets = [(-1, 0, 0), (1, 0, 0), (0, -1, 0), (0, 1, 0), (0, 0, -1), (0, 0, 1)]
    columns_list = []
    for step_x, step_y, step_z in offsets:
        nx = gx + step_x
        ny = gy + step_y
        nz = gz + step_z
        inside = (nx >= 0) & (nx < GRID_X) & (ny >= 0) & (ny < GRID_Y) & (nz >= 0) & (nz < BZ)
        cx = jnp.clip(nx, 0, GRID_X - 1)
        cy = jnp.clip(ny, 0, GRID_Y - 1)
        cz = jnp.clip(nz, 0, BZ - 1)
        other = cx // BX * tiles_y + cy // BY
        place = (cx % BX * BY + cy % BY) * BZ + cz
        ident = other * SLOTS + slot_of[other, place]
        keep = inside & alive & active[cx, cy, cz]
        columns_list.append(jnp.where(keep, ident, -1).reshape(-1))
    return (alive.reshape(-1), jnp.stack(columns_list, axis=1).astype(jnp.int32))


def draw_neighbours(key, part):
    return lattice(key)[1]


def draw_occupancy(key, part):
    alive = lattice(key)[0]
    dice = jax.random.randint(jax.random.fold_in(key, 21), (BRICKS, VOX), 0, 5)
    return (alive[:, None] & (dice < 3)).astype(jnp.int32)


def steps_of(rng, shape, cuts, least, high):
    level = 1.0
    for axis_at, blocks in cuts:
        draws = jax.random.uniform(jax.random.fold_in(jax.random.fold_in(rng, 6), axis_at), (blocks,), jnp.float32, least / len(cuts), high / len(cuts))
        level = level * jnp.repeat(jnp.exp(draws), shape[axis_at] // blocks).reshape((-1,) + (1,) * (len(shape) - 1 - axis_at))
    return level


def noise(own_key, shape, scale, most, cuts=(), held_as=jnp.bfloat16):
    drawn = scale * jax.random.normal(own_key, shape, jnp.float32)
    if cuts:
        drawn = drawn * steps_of(own_key, shape, cuts, -0.22, 0.18)
    return jnp.clip(drawn, -most, most).astype(held_as)


def setup_inputs(seed: int = 0) -> dict:
    key_list = jax.random.split(jax.random.key(seed), 7)
    return {
        "features": noise(key_list[0], (BRICKS, C, VOX), 1.0, 6.0, ((0, 256),)),
        "occupancy": draw_occupancy(jax.random.fold_in(key_list[6], 71), 0),
        "neighbours": draw_neighbours(jax.random.fold_in(key_list[6], 71), 0),
        "w_first": noise(key_list[3], (C, 27 * C), (27 * C) ** -0.5, 0.21875),
        "w_second": noise(key_list[4], (C, 27 * C), (27 * C) ** -0.5, 0.21875),
        "cotangent": noise(key_list[5], (BRICKS, C, VOX), 1.0, 6.0, ((0, 256),)),
    }


def face_planes(field):
    count, chans = (field.shape[0], field.shape[1])
    cube = field.reshape(count, chans, EDGE, EDGE, EDGE)
    faces = [cube[:, :, 0], cube[:, :, -1], cube[:, :, :, 0], cube[:, :, :, -1], cube[:, :, :, :, 0], cube[:, :, :, :, -1]]
    return [face.reshape(count, chans, EDGE * EDGE) for face in faces]

def collect_all(items, neighbours):
    result = []
    for face in range(6):
        ident = neighbours[:, face]
        valid = (ident >= 0).astype(items[0].dtype)
        picked = jnp.take(items[face ^ 1], jnp.maximum(ident, 0), axis=0)
        result.append(picked * valid[:, None, None])
    return result

def padded(field, halos):
    count, chans = (field.shape[0], field.shape[1])
    cube = field.reshape(count, chans, EDGE, EDGE, EDGE)
    cells = jnp.pad(cube, ((0, 0), (0, 0), (1, 1), (1, 1), (1, 1)))
    sheet = [h.astype(field.dtype).reshape(count, chans, EDGE, EDGE) for h in halos]
    cells = cells.at[:, :, 0, 1:-1, 1:-1].set(sheet[0])
    cells = cells.at[:, :, -1, 1:-1, 1:-1].set(sheet[1])
    cells = cells.at[:, :, 1:-1, 0, 1:-1].set(sheet[2])
    cells = cells.at[:, :, 1:-1, -1, 1:-1].set(sheet[3])
    cells = cells.at[:, :, 1:-1, 1:-1, 0].set(sheet[4])
    cells = cells.at[:, :, 1:-1, 1:-1, -1].set(sheet[5])
    return cells

def columns(block):
    count, chans = (block.shape[0], block.shape[1])
    pieces = []
    for first in range(3):
        for second in range(3):
            for third in range(3):
                piece = block[:, :, first:first + EDGE, second:second + EDGE, third:third + EDGE]
                pieces.append(piece.reshape(count, chans, EDGE * EDGE * EDGE))
    return jnp.concatenate(pieces, axis=1)

def conv_blocks(cells, weight, group):
    count = cells.shape[0]
    blocks = cells.reshape((count // group, group) + cells.shape[1:])

    def one_block(block):
        return jnp.einsum('ok,gkv->gov', weight.astype(jnp.float32), columns(block).astype(jnp.float32))
    out = lax.map(one_block, blocks)
    return out.reshape(count, weight.shape[0], -1)

def weight_grad(cells, grad, group):
    count = cells.shape[0]
    blocks = cells.reshape((count // group, group) + cells.shape[1:])
    grads = grad.reshape((count // group, group) + grad.shape[1:])

    def one_block(pair):
        return jnp.einsum('gov,gkv->ok', pair[1].astype(jnp.float32), columns(pair[0]).astype(jnp.float32))
    return lax.optimization_barrier(jnp.sum(lax.map(one_block, (blocks, grads)), axis=0))

def flipped(weight):
    chans = weight.shape[0]
    return weight.reshape(chans, 27, chans)[:, ::-1, :].transpose(2, 1, 0).reshape(chans, 27 * chans)

def reference(features, occupancy, neighbours, w_first, w_second, cotangent):
    group = SLOTS
    mask = occupancy.astype(jnp.float32)[:, None, :]
    x_zero = (features.astype(jnp.float32) * mask).astype(jnp.bfloat16)
    pad_x = padded(x_zero, collect_all(face_planes(x_zero), neighbours))
    pre_one = conv_blocks(pad_x, w_first, group)
    hidden = (jnp.maximum(pre_one, 0.0) * mask).astype(jnp.bfloat16)
    pad_h = padded(hidden, collect_all(face_planes(hidden), neighbours))
    pre_two = conv_blocks(pad_h, w_second, group) + x_zero.astype(jnp.float32)
    result = (jnp.maximum(pre_two, 0.0) * mask).astype(jnp.bfloat16)
    grad_two = jnp.where(pre_two > 0.0, cotangent.astype(jnp.float32) * mask, 0.0).astype(jnp.bfloat16)
    scale = 1.0 / math.sqrt(BRICKS * VOX)
    grad_second = weight_grad(pad_h, grad_two, group) * scale
    pad_g = padded(grad_two, collect_all(face_planes(grad_two), neighbours))
    dhidden = conv_blocks(pad_g, flipped(w_second), group)
    grad_one = jnp.where(pre_one > 0.0, dhidden * mask, 0.0).astype(jnp.bfloat16)
    grad_first = weight_grad(pad_x, grad_one, group) * scale
    pad_one = padded(grad_one, collect_all(face_planes(grad_one), neighbours))
    dinput = conv_blocks(pad_one, flipped(w_first), group) + grad_two.astype(jnp.float32)
    grad_features = (dinput * mask).astype(jnp.bfloat16)
    return (result, grad_features, grad_first, grad_second)
```

```python
import functools
import math

import jax
import jax.numpy as jnp
import numpy as np
from jax import lax
from jax.experimental import pallas as pl
from jax.experimental.pallas import tpu as pltpu
from jax.sharding import PartitionSpec as P

EDGE = 8
LANES = 128
PITCH = 10
SLOTS = 6
CHANS = 32
INNER = EDGE * LANES
WHOLE = (EDGE + 2) * LANES
BF16 = jnp.bfloat16
F32 = jnp.float32
VMEM_LIMIT = 24 * 1024 * 1024


def lane_of(row, col):
    return (row + 1) * PITCH + col + 1


def spread_matrix():
    out = np.zeros((2 * EDGE * EDGE, 2 * LANES), np.float32)
    for half in range(2):
        for row in range(EDGE):
            for col in range(EDGE):
                out[half * 64 + row * EDGE + col, half * LANES + lane_of(row, col)] = 1
    return out


def face_matrices():
    pick = np.zeros((INNER, 256), np.float32)
    put = np.zeros((256, INNER), np.float32)
    for plane in range(EDGE):
        base = plane * LANES
        for at in range(EDGE):
            col = plane * EDGE + at
            pick[base + lane_of(EDGE - 1, at), col] = 1
            pick[base + lane_of(0, at), 64 + col] = 1
            pick[base + lane_of(at, EDGE - 1), 128 + col] = 1
            pick[base + lane_of(at, 0), 192 + col] = 1
            put[col, base + lane_of(-1, at)] = 1
            put[64 + col, base + lane_of(EDGE, at)] = 1
            put[128 + col, base + lane_of(at, -1)] = 1
            put[192 + col, base + lane_of(at, EDGE)] = 1
    return pick, put


SPREAD = spread_matrix()
PICK, PUT = face_matrices()


def dot(lhs, rhs):
    return jnp.dot(lhs, rhs, preferred_element_type=F32)


def spread(field, matrix):
    return [dot(field[:, at * LANES : (at + 1) * LANES], matrix) for at in range(4)]


def emit_faces(inner_ref, pick_ref, low_ref, high_ref, side_ref):
    low_ref[...] = inner_ref[:, :, :LANES]
    high_ref[...] = inner_ref[:, :, INNER - LANES :]
    flat = inner_ref[...].reshape(SLOTS * CHANS, INNER)
    side_ref[...] = dot(flat, pick_ref[...]).astype(BF16).reshape(SLOTS, CHANS, 256)


def build_cells(cells_ref, sheet_ref, inner_ref, side_ref, remote_refs, put_ref, neighbours_ref, base):
    lane = lax.broadcasted_iota(jnp.int32, (1, LANES), 1)
    lower = (lane < 64).astype(F32).astype(BF16)
    upper = (lane >= 64).astype(F32).astype(BF16)
    zero = jnp.zeros((CHANS, LANES), BF16)

    def picked(slot, face, local, remote_ref):
        ident = neighbours_ref[slot, face]
        place = lax.rem(jnp.maximum(ident, 0), SLOTS)
        value = local(place)
        if remote_ref is not None:
            here = (ident >= base) & (ident < base + SLOTS)
            value = jnp.where(here, value, remote_ref[place])
        return jnp.where(ident >= 0, value, zero)

    rows_ref, cols_ref, before_ref, after_ref = remote_refs
    for slot in range(SLOTS):
        cells_ref[slot, :, :LANES] = picked(
            slot, 0, lambda at: inner_ref[at, :, INNER - LANES :], rows_ref
        )
        cells_ref[slot, :, WHOLE - LANES :] = picked(
            slot, 1, lambda at: inner_ref[at, :, :LANES], cols_ref
        )
        sides = lambda at: side_ref[at, :, :LANES]
        ends = lambda at: side_ref[at, :, LANES:]
        rows = pl.ds(slot * CHANS, CHANS)
        sheet_ref[rows, :LANES] = (
            picked(slot, 2, sides, before_ref) * lower + picked(slot, 3, sides, after_ref) * upper
        )
        sheet_ref[rows, LANES:] = (
            picked(slot, 4, ends, None) * lower + picked(slot, 5, ends, None) * upper
        )
    halo = dot(sheet_ref[...], put_ref[...]).astype(BF16).reshape(SLOTS, CHANS, INNER)
    cells_ref[:, :, LANES : LANES + INNER] = inner_ref[...] + halo


def shift_planes(columns_ref, cells_ref, slot):
    for plane in range(EDGE + 2):
        span = slice(plane * LANES, (plane + 1) * LANES)
        tile = cells_ref[slot, :, span]
        for tap in range(9):
            shift = (tap // 3 - 1) * PITCH + tap % 3 - 1
            moved = tile if shift == 0 else pltpu.roll(tile, (-shift) % LANES, 1)
            columns_ref[tap * CHANS : (tap + 1) * CHANS, span] = moved


def stacked(weight):
    return jnp.concatenate([weight[:, at * 288 : (at + 1) * 288] for at in range(3)], axis=0)


def convolve(columns_ref, weight):
    raw = dot(weight, columns_ref[...])
    return (
        raw[:CHANS, :INNER]
        + raw[CHANS : 2 * CHANS, LANES : LANES + INNER]
        + raw[2 * CHANS :, 2 * LANES :]
    )


def enter_kernel(features_ref, occupancy_ref, spread_ref, pick_ref, inner_ref, mask_ref, low_ref, high_ref, side_ref):
    mask = occupancy_ref[...].astype(F32).astype(BF16)
    matrix = spread_ref[...]
    for at, part in enumerate(spread(mask, matrix)):
        mask_ref[:, at * 256 : (at + 1) * 256] = part
    masked = jnp.concatenate(
        [features_ref[slot] * mask[slot : slot + 1, :] for slot in range(SLOTS)], axis=0
    )
    for at, part in enumerate(spread(masked, matrix)):
        inner_ref[:, :, at * 256 : (at + 1) * 256] = part.astype(BF16).reshape(SLOTS, CHANS, 256)
    emit_faces(inner_ref, pick_ref, low_ref, high_ref, side_ref)


def spread_kernel(cotangent_ref, mask_ref, spread_ref, out_ref):
    flat = cotangent_ref[...].reshape(SLOTS * CHANS, 512)
    for at, part in enumerate(spread(flat, spread_ref[...])):
        span = slice(at * 256, (at + 1) * 256)
        for slot in range(SLOTS):
            out_ref[slot, :, span] = (
                part[slot * CHANS : (slot + 1) * CHANS] * mask_ref[slot : slot + 1, span]
            ).astype(BF16)


def first_kernel(neighbours_ref, base_ref, inner_ref, side_ref, r0, r1, r2, r3, put_ref, pick_ref, weight_ref, mask_ref,
                 cells_ref, hidden_ref, low_ref, high_ref, hidden_side_ref, sheet_ref, columns_ref):
    build_cells(cells_ref, sheet_ref, inner_ref, side_ref, (r0, r1, r2, r3), put_ref, neighbours_ref, base_ref[0])
    weight = stacked(weight_ref[...])
    for slot in range(SLOTS):
        buffer = columns_ref.at[slot % 2]
        shift_planes(buffer, cells_ref, slot)
        pre = convolve(buffer, weight)
        hidden_ref[slot] = (jnp.maximum(pre, 0.0) * mask_ref[slot : slot + 1, :]).astype(BF16)
    emit_faces(hidden_ref, pick_ref, low_ref, high_ref, hidden_side_ref)


def pack_rows(inner, gather):
    return [dot(inner[:, at * 256 : (at + 1) * 256], gather) for at in range(4)]


def second_kernel(neighbours_ref, base_ref, inner_ref, side_ref, r0, r1, r2, r3, put_ref, pick_ref, gather_ref, weight_ref,
                  mask_ref, skip_ref, cotangent_ref,
                  cells_ref, result_ref, grad_ref, low_ref, high_ref, grad_side_ref, sheet_ref, columns_ref, wide_ref):
    build_cells(cells_ref, sheet_ref, inner_ref, side_ref, (r0, r1, r2, r3), put_ref, neighbours_ref, base_ref[0])
    weight = stacked(weight_ref[...])
    for slot in range(SLOTS):
        buffer = columns_ref.at[slot % 2]
        shift_planes(buffer, cells_ref, slot)
        pre = convolve(buffer, weight) + skip_ref[slot].astype(F32)
        wide_ref[slot] = (jnp.maximum(pre, 0.0) * mask_ref[slot : slot + 1, :]).astype(BF16)
        grad_ref[slot] = jnp.where(pre > 0.0, cotangent_ref[slot].astype(F32), 0.0).astype(BF16)
    emit_faces(grad_ref, pick_ref, low_ref, high_ref, grad_side_ref)
    flat = wide_ref[...].reshape(SLOTS * CHANS, INNER)
    for at, part in enumerate(pack_rows(flat, gather_ref[...])):
        result_ref[:, :, at * LANES : (at + 1) * LANES] = part.astype(BF16).reshape(SLOTS, CHANS, LANES)


def third_kernel(neighbours_ref, base_ref, inner_ref, side_ref, r0, r1, r2, r3, put_ref, pick_ref, weight_ref, mask_ref,
                 hidden_ref, grad_ref, low_ref, high_ref, grad_side_ref, cells_ref, sheet_ref, columns_ref):
    build_cells(cells_ref, sheet_ref, inner_ref, side_ref, (r0, r1, r2, r3), put_ref, neighbours_ref, base_ref[0])
    weight = weight_ref[...]
    for slot in range(SLOTS):
        buffer = columns_ref.at[slot % 2]
        shift_planes(buffer, cells_ref, slot)
        grad = convolve(buffer, weight) * mask_ref[slot : slot + 1, :]
        grad_ref[slot] = jnp.where(hidden_ref[slot].astype(F32) > 0.0, grad, 0.0).astype(BF16)
    emit_faces(grad_ref, pick_ref, low_ref, high_ref, grad_side_ref)


def last_kernel(neighbours_ref, base_ref, inner_ref, side_ref, r0, r1, r2, r3, put_ref, gather_ref, weight_ref, mask_ref,
                grad_ref, out_ref, cells_ref, sheet_ref, columns_ref, wide_ref):
    build_cells(cells_ref, sheet_ref, inner_ref, side_ref, (r0, r1, r2, r3), put_ref, neighbours_ref, base_ref[0])
    weight = weight_ref[...]
    for slot in range(SLOTS):
        buffer = columns_ref.at[slot % 2]
        shift_planes(buffer, cells_ref, slot)
        grad = convolve(buffer, weight) + grad_ref[slot].astype(F32)
        wide_ref[slot] = (grad * mask_ref[slot : slot + 1, :]).astype(BF16)
    flat = wide_ref[...].reshape(SLOTS * CHANS, INNER)
    for at, part in enumerate(pack_rows(flat, gather_ref[...])):
        out_ref[:, :, at * LANES : (at + 1) * LANES] = part.astype(BF16).reshape(SLOTS, CHANS, LANES)


def weight_kernel(cells_ref, grad_ref, out_ref, columns_ref, grads_ref):
    grads_ref[...] = jnp.zeros_like(grads_ref)
    total = jnp.zeros((9 * CHANS, 3 * CHANS), F32)
    for slot in range(SLOTS):
        buffer = columns_ref.at[slot % 2]
        shift_planes(buffer, cells_ref, slot)
        spot = grads_ref.at[slot % 2]
        for at in range(3):
            spot[at * CHANS : (at + 1) * CHANS, at * LANES : at * LANES + INNER] = grad_ref[slot]
        total = total + lax.dot_general(
            buffer[...], spot[...], (((1,), (1,)), ((), ())), preferred_element_type=F32
        )
    turned = total.T
    for at in range(3):
        out_ref[:, at * 288 : (at + 1) * 288] = turned[at * CHANS : (at + 1) * CHANS]


def shape(dims, dtype=BF16):
    return jax.ShapeDtypeStruct(dims, dtype)


FIELD = (SLOTS, CHANS, 512)
INSIDE = (SLOTS, CHANS, INNER)
CELLS = (SLOTS, CHANS, WHOLE)
FACE = (SLOTS, CHANS, LANES)
SIDE = (SLOTS, CHANS, 2 * LANES)
FACES = [shape(FACE), shape(FACE), shape(SIDE)]
SCRATCH = [pltpu.VMEM((SLOTS * CHANS, 256), BF16), pltpu.VMEM((2, 9 * CHANS, WHOLE), BF16)]


def call(kernel, outs, scratch, scalars, flops, name):
    def run(*args):
        specs = [
            pl.BlockSpec(memory_space=pltpu.SMEM if at < scalars else pltpu.VMEM)
            for at in range(len(args))
        ]
        moved = sum(a.size * a.dtype.itemsize for a in args)
        moved += sum(math.prod(o.shape) * o.dtype.itemsize for o in outs)
        result = pl.pallas_call(
            kernel,
            out_shape=outs,
            in_specs=specs,
            out_specs=[pl.BlockSpec(memory_space=pltpu.VMEM)] * len(outs),
            scratch_shapes=scratch,
            compiler_params=pltpu.CompilerParams(vmem_limit_bytes=VMEM_LIMIT),
            cost_estimate=pl.CostEstimate(flops=flops, bytes_accessed=moved, transcendentals=0),
            name=name,
        )(*args)
        return result

    return run


def passed_along(value, axis, steps):
    count = lax.axis_size(axis)
    first, last = (max(0, -steps), min(count, count - steps))
    return lax.ppermute(value, axis, [(source, source + steps) for source in range(first, last)])


def exchanged(low, high, side):
    return (
        passed_along(high, "tx", 1),
        passed_along(low, "tx", -1),
        passed_along(side[:, :, :LANES], "ty", 1),
        passed_along(side[:, :, :LANES], "ty", -1),
    )


def swapped(value, axis, bit):
    count = lax.axis_size(axis)
    return lax.ppermute(value, axis, [(at, at ^ bit) for at in range(count)])


def summed(first, second):
    odd = lax.rem(lax.axis_index("ty"), 2) == 1
    kept = jnp.where(odd, second, first)
    total = kept + swapped(jnp.where(odd, first, second), "ty", 1)
    for axis, bit in (("ty", 2), ("ty", 4), ("ty", 8), ("ty", 16), ("tx", 1), ("tx", 2), ("tx", 4)):
        mine = total.astype(BF16)
        total = mine.astype(F32) + swapped(mine, axis, bit).astype(F32)
    other = swapped(total, "ty", 1)
    return jnp.where(odd, other, total), jnp.where(odd, total, other)


def turned(weight):
    taps = weight.reshape(CHANS, 3, 3, 3, CHANS)[:, ::-1, ::-1, ::-1]
    return taps.transpose(1, 4, 2, 3, 0).reshape(3 * CHANS, 9 * CHANS)


CONV_FLOPS = 2 * 96 * 288 * WHOLE * SLOTS


def body(features, occupancy, neighbours, w_first, w_second, cotangent):
    myself = lax.axis_index("tx") * lax.axis_size("ty") + lax.axis_index("ty")
    base = (myself * SLOTS).astype(jnp.int32).reshape(1)
    widen = jnp.asarray(SPREAD, BF16)
    narrow = jnp.asarray(SPREAD.T, BF16)
    pick = jnp.asarray(PICK, BF16)
    put = jnp.asarray(PUT, BF16)
    x_inner, mask, low, high, side = call(
        enter_kernel, [shape(INSIDE), shape((SLOTS, INNER), F32)] + FACES, [], 0, 2 * 192 * 512 * 1024, "enter"
    )(features, occupancy, widen, pick)
    remote = exchanged(low, high, side)
    (cot_inner,) = call(spread_kernel, [shape(INSIDE)], [], 0, 2 * 192 * 512 * 256, "spread")(
        cotangent, mask, widen
    )
    back_second, back_first = turned(w_second), turned(w_first)
    x_cells, hidden, low, high, hidden_side = call(
        first_kernel, [shape(CELLS), shape(INSIDE)] + FACES, SCRATCH, 2, CONV_FLOPS, "first"
    )(neighbours, base, x_inner, side, *remote, put, pick, w_first, mask)
    remote = exchanged(low, high, hidden_side)
    hidden_cells, result, grad_two, low, high, grad_side = call(
        second_kernel,
        [shape(CELLS), shape(FIELD), shape(INSIDE)] + FACES,
        SCRATCH + [pltpu.VMEM(INSIDE, BF16)],
        2,
        CONV_FLOPS,
        "second",
    )(neighbours, base, hidden, hidden_side, *remote, put, pick, narrow, w_second, mask, x_inner, cot_inner)
    remote = exchanged(low, high, grad_side)
    weight_scratch = [SCRATCH[1], pltpu.VMEM((2, 3 * CHANS, WHOLE), BF16)]
    weight_call = call(weight_kernel, [shape((CHANS, 27 * CHANS), F32)], weight_scratch, 0, CONV_FLOPS, "weights")
    (term_second,) = weight_call(hidden_cells, grad_two)
    grad_one, low, high, one_side = call(
        third_kernel, [shape(INSIDE)] + FACES, [pltpu.VMEM(CELLS, BF16)] + SCRATCH, 2, CONV_FLOPS, "third"
    )(neighbours, base, grad_two, grad_side, *remote, put, pick, back_second, mask, hidden)
    remote = exchanged(low, high, one_side)
    (term_first,) = weight_call(x_cells, grad_one)
    (grad_features,) = call(
        last_kernel,
        [shape(FIELD)],
        [pltpu.VMEM(CELLS, BF16)] + SCRATCH + [pltpu.VMEM(INSIDE, BF16)],
        2,
        CONV_FLOPS,
        "last",
    )(neighbours, base, grad_one, one_side, *remote, put, narrow, back_first, mask, grad_two)
    total_first, total_second = summed(term_first, term_second)
    scale = 1.0 / math.sqrt(SLOTS * lax.axis_size("tx") * lax.axis_size("ty") * EDGE**3)
    return (result, grad_features, total_first * scale, total_second * scale)


def solution(mesh):
    return jax.shard_map(
        body,
        mesh=mesh,
        in_specs=(
            P(("tx", "ty"), None, None),
            P(("tx", "ty"), None),
            P(("tx", "ty"), None),
            P(),
            P(),
            P(("tx", "ty"), None, None),
        ),
        out_specs=(P(("tx", "ty"), None, None), P(("tx", "ty"), None, None), P(), P()),
        check_vma=False,
    )
```

```python
import functools
import math

import jax
import jax.numpy as jnp
import numpy as np
from jax import lax
from jax.experimental import pallas as pl
from jax.experimental.pallas import tpu as pltpu
from jax.sharding import PartitionSpec as P

EDGE = 8
LANES = 128
PITCH = 10
SLOTS = 6
CHANS = 32
INNER = EDGE * LANES
WHOLE = (EDGE + 2) * LANES
BF16 = jnp.bfloat16
F32 = jnp.float32
VMEM_LIMIT = 16 * 1024 * 1024


def lane_of(row, col):
    return (row + 1) * PITCH + col + 1


def spread_matrix():
    out = np.zeros((2 * EDGE * EDGE, 2 * LANES), np.float32)
    for half in range(2):
        for row in range(EDGE):
            for col in range(EDGE):
                out[half * 64 + row * EDGE + col, half * LANES + lane_of(row, col)] = 1
    return out


def face_matrices():
    pick = np.zeros((INNER, 256), np.float32)
    put = np.zeros((256, INNER), np.float32)
    for plane in range(EDGE):
        base = plane * LANES
        for at in range(EDGE):
            col = plane * EDGE + at
            pick[base + lane_of(EDGE - 1, at), col] = 1
            pick[base + lane_of(0, at), 64 + col] = 1
            pick[base + lane_of(at, EDGE - 1), 128 + col] = 1
            pick[base + lane_of(at, 0), 192 + col] = 1
            put[col, base + lane_of(-1, at)] = 1
            put[64 + col, base + lane_of(EDGE, at)] = 1
            put[128 + col, base + lane_of(at, -1)] = 1
            put[192 + col, base + lane_of(at, EDGE)] = 1
    return pick, put


SPREAD = spread_matrix()
PICK, PUT = face_matrices()


def dot(lhs, rhs):
    return jnp.dot(lhs, rhs, preferred_element_type=F32)


def spread(field, matrix):
    return [dot(field[:, at * LANES : (at + 1) * LANES], matrix) for at in range(4)]


def emit_faces(place_ref, inner_ref, pick_ref, even_ref, odd_ref, side_ref):
    raised = place_ref[1] == 1
    low = inner_ref[:, :, :LANES]
    high = inner_ref[:, :, INNER - LANES :]
    even_ref[...] = jnp.where(raised, low, high)
    odd_ref[...] = jnp.where(raised, high, low)
    flat = inner_ref[...].reshape(SLOTS * CHANS, INNER)
    side_ref[...] = dot(flat, pick_ref[...]).astype(BF16).reshape(SLOTS, CHANS, 256)


def build_cells(cells_ref, sheet_ref, inner_ref, side_ref, remote_refs, put_ref, neighbours_ref, place_ref):
    base = place_ref[0]
    lane = lax.broadcasted_iota(jnp.int32, (1, LANES), 1)
    lower = (lane < 64).astype(F32).astype(BF16)
    upper = (lane >= 64).astype(F32).astype(BF16)
    zero = jnp.zeros((CHANS, LANES), BF16)

    x_even_ref, x_odd_ref, y_even_ref, y_odd_ref = remote_refs
    pairs = ((x_odd_ref, x_even_ref), (x_even_ref, x_odd_ref), (y_odd_ref, y_even_ref), (y_even_ref, y_odd_ref))

    def picked(slot, face, local):
        ident = neighbours_ref[slot, face]
        place = lax.rem(jnp.maximum(ident, 0), SLOTS)
        value = local(place)
        if face < 4:
            here = (ident >= base) & (ident < base + SLOTS)
            settled, raised = pairs[face]
            distant = jnp.where(place_ref[1 + face // 2] == 1, raised[place], settled[place])
            value = jnp.where(here, value, distant)
        return jnp.where(ident >= 0, value, zero)

    for slot in range(SLOTS):
        cells_ref[slot, :, :LANES] = picked(
            slot, 0, lambda at: inner_ref[at, :, INNER - LANES :]
        )
        cells_ref[slot, :, WHOLE - LANES :] = picked(
            slot, 1, lambda at: inner_ref[at, :, :LANES]
        )
        sides = lambda at: side_ref[at, :, :LANES]
        ends = lambda at: side_ref[at, :, LANES:]
        rows = pl.ds(slot * CHANS, CHANS)
        sheet_ref[rows, :LANES] = (
            picked(slot, 2, sides) * lower + picked(slot, 3, sides) * upper
        )
        sheet_ref[rows, LANES:] = (
            picked(slot, 4, ends) * lower + picked(slot, 5, ends) * upper
        )
    halo = dot(sheet_ref[...], put_ref[...]).astype(BF16).reshape(SLOTS, CHANS, INNER)
    cells_ref[:, :, LANES : LANES + INNER] = inner_ref[...] + halo


def shift_planes(columns_ref, cells_ref, slot):
    for plane in range(EDGE + 2):
        span = slice(plane * LANES, (plane + 1) * LANES)
        tile = cells_ref[slot, :, span]
        for tap in range(9):
            shift = (tap // 3 - 1) * PITCH + tap % 3 - 1
            moved = tile if shift == 0 else pltpu.roll(tile, (-shift) % LANES, 1)
            columns_ref[tap * CHANS : (tap + 1) * CHANS, span] = moved


def stacked(weight):
    return jnp.concatenate([weight[:, at * 288 : (at + 1) * 288] for at in range(3)], axis=0)


def convolve(columns_ref, weight):
    raw = dot(weight, columns_ref[...])
    return (
        raw[:CHANS, :INNER]
        + raw[CHANS : 2 * CHANS, LANES : LANES + INNER]
        + raw[2 * CHANS :, 2 * LANES :]
    )


def enter_kernel(place_ref, features_hbm, occupancy_hbm, spread_hbm, pick_hbm, inner_ref, mask_ref, even_ref, odd_ref, side_ref,
                 features_ref, occupancy_ref, spread_ref, pick_ref, sems):
    loads = [
        pltpu.make_async_copy(source, target, sems.at[at])
        for at, (source, target) in enumerate(
            ((occupancy_hbm, occupancy_ref), (spread_hbm, spread_ref), (features_hbm, features_ref), (pick_hbm, pick_ref))
        )
    ]
    for load in loads:
        load.start()
    for load in loads[:3]:
        load.wait()
    mask = occupancy_ref[...].astype(F32).astype(BF16)
    matrix = spread_ref[...]
    for at, part in enumerate(spread(mask, matrix)):
        mask_ref[:, at * 256 : (at + 1) * 256] = part
    masked = jnp.concatenate(
        [features_ref[slot] * mask[slot : slot + 1, :] for slot in range(SLOTS)], axis=0
    )
    for at, part in enumerate(spread(masked, matrix)):
        inner_ref[:, :, at * 256 : (at + 1) * 256] = part.astype(BF16).reshape(SLOTS, CHANS, 256)
    loads[3].wait()
    emit_faces(place_ref, inner_ref, pick_ref, even_ref, odd_ref, side_ref)


def turned(weight):
    taps = weight.astype(F32).T.astype(BF16)
    rows = []
    for first in range(3):
        blocks = []
        for rest in range(9):
            tap = 26 - first * 9 - rest
            blocks.append(taps[tap * CHANS : (tap + 1) * CHANS])
        rows.append(jnp.concatenate(blocks, axis=1))
    return jnp.concatenate(rows, axis=0)


def turn_kernel(first_ref, second_ref, back_first_ref, back_second_ref):
    back_first_ref[...] = turned(first_ref[...])
    back_second_ref[...] = turned(second_ref[...])


def spread_kernel(cotangent_ref, mask_ref, spread_ref, out_ref):
    flat = cotangent_ref[...].reshape(SLOTS * CHANS, 512)
    for at, part in enumerate(spread(flat, spread_ref[...])):
        span = slice(at * 256, (at + 1) * 256)
        for slot in range(SLOTS):
            out_ref[slot, :, span] = (
                part[slot * CHANS : (slot + 1) * CHANS] * mask_ref[slot : slot + 1, span]
            ).astype(BF16)


def first_kernel(neighbours_ref, place_ref, inner_ref, side_ref, r0, r1, r2, r3, put_ref, pick_ref, weight_ref, mask_ref,
                 cells_ref, hidden_ref, even_ref, odd_ref, hidden_side_ref, sheet_ref, columns_ref):
    build_cells(cells_ref, sheet_ref, inner_ref, side_ref, (r0, r1, r2, r3), put_ref, neighbours_ref, place_ref)
    weight = stacked(weight_ref[...])
    for slot in range(SLOTS):
        buffer = columns_ref.at[slot % 2]
        shift_planes(buffer, cells_ref, slot)
        pre = convolve(buffer, weight)
        hidden_ref[slot] = (jnp.maximum(pre, 0.0) * mask_ref[slot : slot + 1, :]).astype(BF16)
    emit_faces(place_ref, hidden_ref, pick_ref, even_ref, odd_ref, hidden_side_ref)


def pack_rows(inner, gather):
    return [dot(inner[:, at * 256 : (at + 1) * 256], gather) for at in range(4)]


def second_kernel(neighbours_ref, place_ref, inner_ref, side_ref, r0, r1, r2, r3, put_ref, pick_ref, gather_ref, weight_ref,
                  mask_ref, skip_ref, cotangent_ref,
                  cells_ref, result_ref, grad_ref, even_ref, odd_ref, grad_side_ref, sheet_ref, columns_ref, wide_ref):
    build_cells(cells_ref, sheet_ref, inner_ref, side_ref, (r0, r1, r2, r3), put_ref, neighbours_ref, place_ref)
    weight = stacked(weight_ref[...])
    for slot in range(SLOTS):
        buffer = columns_ref.at[slot % 2]
        shift_planes(buffer, cells_ref, slot)
        pre = convolve(buffer, weight) + skip_ref[slot].astype(F32)
        wide_ref[slot] = (jnp.maximum(pre, 0.0) * mask_ref[slot : slot + 1, :]).astype(BF16)
        grad_ref[slot] = jnp.where(pre > 0.0, cotangent_ref[slot].astype(F32), 0.0).astype(BF16)
    emit_faces(place_ref, grad_ref, pick_ref, even_ref, odd_ref, grad_side_ref)
    flat = wide_ref[...].reshape(SLOTS * CHANS, INNER)
    for at, part in enumerate(pack_rows(flat, gather_ref[...])):
        result_ref[:, :, at * LANES : (at + 1) * LANES] = part.astype(BF16).reshape(SLOTS, CHANS, LANES)


def third_kernel(neighbours_ref, place_ref, inner_ref, side_ref, r0, r1, r2, r3, put_ref, pick_ref, weight_ref, mask_ref,
                 hidden_ref, grad_ref, even_ref, odd_ref, grad_side_ref, cells_ref, sheet_ref, columns_ref):
    build_cells(cells_ref, sheet_ref, inner_ref, side_ref, (r0, r1, r2, r3), put_ref, neighbours_ref, place_ref)
    weight = weight_ref[...]
    for slot in range(SLOTS):
        buffer = columns_ref.at[slot % 2]
        shift_planes(buffer, cells_ref, slot)
        grad = convolve(buffer, weight) * mask_ref[slot : slot + 1, :]
        grad_ref[slot] = jnp.where(hidden_ref[slot].astype(F32) > 0.0, grad, 0.0).astype(BF16)
    emit_faces(place_ref, grad_ref, pick_ref, even_ref, odd_ref, grad_side_ref)


def last_kernel(neighbours_ref, place_ref, inner_ref, side_ref, r0, r1, r2, r3, put_ref, gather_ref, weight_ref, mask_ref,
                grad_ref, out_ref, cells_ref, sheet_ref, columns_ref, wide_ref):
    build_cells(cells_ref, sheet_ref, inner_ref, side_ref, (r0, r1, r2, r3), put_ref, neighbours_ref, place_ref)
    weight = weight_ref[...]
    for slot in range(SLOTS):
        buffer = columns_ref.at[slot % 2]
        shift_planes(buffer, cells_ref, slot)
        grad = convolve(buffer, weight) + grad_ref[slot].astype(F32)
        wide_ref[slot] = (grad * mask_ref[slot : slot + 1, :]).astype(BF16)
    flat = wide_ref[...].reshape(SLOTS * CHANS, INNER)
    for at, part in enumerate(pack_rows(flat, gather_ref[...])):
        out_ref[:, :, at * LANES : (at + 1) * LANES] = part.astype(BF16).reshape(SLOTS, CHANS, LANES)


def weight_kernel(cells_ref, grad_ref, out_ref, columns_ref, grads_ref):
    grads_ref[...] = jnp.zeros_like(grads_ref)
    total = jnp.zeros((9 * CHANS, 3 * CHANS), F32)
    for slot in range(SLOTS):
        buffer = columns_ref.at[slot % 2]
        shift_planes(buffer, cells_ref, slot)
        spot = grads_ref.at[slot % 2]
        for at in range(3):
            spot[at * CHANS : (at + 1) * CHANS, at * LANES : at * LANES + INNER] = grad_ref[slot]
        total = total + lax.dot_general(
            buffer[...], spot[...], (((1,), (1,)), ((), ())), preferred_element_type=F32
        )
    turned = total.T
    for at in range(3):
        out_ref[:, at * 288 : (at + 1) * 288] = turned[at * CHANS : (at + 1) * CHANS]


def shape(dims, dtype=BF16):
    return jax.ShapeDtypeStruct(dims, dtype)


FIELD = (SLOTS, CHANS, 512)
INSIDE = (SLOTS, CHANS, INNER)
CELLS = (SLOTS, CHANS, WHOLE)
FACE = (SLOTS, CHANS, LANES)
SIDE = (SLOTS, CHANS, 2 * LANES)
FACES = [shape(FACE), shape(FACE), shape(SIDE)]
SCRATCH = [pltpu.VMEM((SLOTS * CHANS, 256), BF16), pltpu.VMEM((2, 9 * CHANS, WHOLE), BF16)]


def call(kernel, outs, scratch, scalars, flops, name, space=pltpu.VMEM):
    def run(*args):
        specs = [
            pl.BlockSpec(memory_space=pltpu.SMEM if at < scalars else space)
            for at in range(len(args))
        ]
        moved = sum(a.size * a.dtype.itemsize for a in args)
        moved += sum(math.prod(o.shape) * o.dtype.itemsize for o in outs)
        result = pl.pallas_call(
            kernel,
            out_shape=outs,
            in_specs=specs,
            out_specs=[pl.BlockSpec(memory_space=pltpu.VMEM)] * len(outs),
            scratch_shapes=scratch,
            compiler_params=pltpu.CompilerParams(vmem_limit_bytes=VMEM_LIMIT),
            cost_estimate=pl.CostEstimate(flops=flops, bytes_accessed=moved, transcendentals=0),
            name=name,
        )(*args)
        return result

    return run


def swapped(value, axis, bit):
    count = lax.axis_size(axis)
    return lax.ppermute(value, axis, [(at, at ^ bit) for at in range(count)])


def paired(value, axis, odd):
    count = lax.axis_size(axis)
    if not odd:
        return swapped(value, axis, 1)
    return lax.ppermute(
        value, axis, [(at, (at + 1 if at % 2 else at - 1) % count) for at in range(count)]
    )


HOPS = (("tx", 0), ("tx", 1), ("ty", 0), ("ty", 1))


def exchanged(even, odd, side):
    sent = (even, odd, side[:, :, :LANES], side[:, :, :LANES])
    return [paired(value, axis, turn) for value, (axis, turn) in zip(sent, HOPS)]


CONV_FLOPS = 2 * 96 * 288 * WHOLE * SLOTS


def body(features, occupancy, neighbours, w_first, w_second, cotangent):
    row, col = lax.axis_index("tx"), lax.axis_index("ty")
    base = (row * lax.axis_size("ty") + col) * SLOTS
    place = jnp.stack([base, row % 2, col % 2]).astype(jnp.int32)
    widen = jnp.asarray(SPREAD, BF16)
    narrow = jnp.asarray(SPREAD.T, BF16)
    pick = jnp.asarray(PICK, BF16)
    put = jnp.asarray(PUT, BF16)
    enter_scratch = [
        pltpu.VMEM(FIELD, BF16),
        pltpu.VMEM((SLOTS, 512), jnp.int32),
        pltpu.VMEM(SPREAD.shape, BF16),
        pltpu.VMEM(PICK.shape, BF16),
        pltpu.SemaphoreType.DMA((4,)),
    ]
    x_inner, mask, even, odd, side = call(
        enter_kernel, [shape(INSIDE), shape((SLOTS, INNER), F32)] + FACES, enter_scratch, 1, 2 * 192 * 512 * 1024, "enter",
        pltpu.HBM,
    )(place, features, occupancy, widen, pick)
    remote = exchanged(even, odd, side)
    (cot_inner,) = call(spread_kernel, [shape(INSIDE)], [], 0, 2 * 192 * 512 * 256, "spread")(
        cotangent, mask, widen
    )
    back_first, back_second = call(
        turn_kernel, [shape((3 * CHANS, 9 * CHANS))] * 2, [], 0, 1 << 20, "turn"
    )(w_first, w_second)
    x_cells, hidden, even, odd, hidden_side = call(
        first_kernel, [shape(CELLS), shape(INSIDE)] + FACES, SCRATCH, 2, CONV_FLOPS, "first"
    )(neighbours, place, x_inner, side, *remote, put, pick, w_first, mask)
    remote = exchanged(even, odd, hidden_side)
    hidden_cells, result, grad_two, even, odd, grad_side = call(
        second_kernel,
        [shape(CELLS), shape(FIELD), shape(INSIDE)] + FACES,
        SCRATCH + [pltpu.VMEM(INSIDE, BF16)],
        2,
        CONV_FLOPS,
        "second",
    )(neighbours, place, hidden, hidden_side, *remote, put, pick, narrow, w_second, mask, x_inner, cot_inner)
    remote = exchanged(even, odd, grad_side)
    weight_scratch = [SCRATCH[1], pltpu.VMEM((2, 3 * CHANS, WHOLE), BF16)]
    weight_call = call(weight_kernel, [shape((CHANS, 27 * CHANS), F32)], weight_scratch, 0, CONV_FLOPS, "weights")
    (term_second,) = weight_call(hidden_cells, grad_two)
    grad_one, even, odd, one_side = call(
        third_kernel, [shape(INSIDE)] + FACES, [pltpu.VMEM(CELLS, BF16)] + SCRATCH, 2, CONV_FLOPS, "third"
    )(neighbours, place, grad_two, grad_side, *remote, put, pick, back_second, mask, hidden)
    (term_first,) = weight_call(x_cells, grad_one)
    sent = (even, odd, one_side[:, :, :LANES], one_side[:, :, :LANES])
    late = col % 2 == 1
    total = jnp.where(late, term_second, term_first) + swapped(
        jnp.where(late, term_first, term_second), "ty", 1
    )
    remote = []
    for step, (axis, bit) in enumerate(
        (("ty", 2), ("ty", 4), ("ty", 8), ("ty", 16), ("tx", 1), ("tx", 2), ("tx", 4))
    ):
        mine = total.astype(BF16)
        if 1 <= step <= 4:
            mine, remote[-1] = lax.optimization_barrier((mine, remote[-1]))
        if step < 4:
            mine, value = lax.optimization_barrier((mine, sent[step]))
            remote.append(paired(value, *HOPS[step]))
        if step == 5:
            mine, remote = lax.optimization_barrier((mine, remote))
            (grad_features,) = call(
                last_kernel,
                [shape(FIELD)],
                [pltpu.VMEM(CELLS, BF16)] + SCRATCH + [pltpu.VMEM(INSIDE, BF16)],
                2,
                CONV_FLOPS,
                "last",
            )(neighbours, place, grad_one, one_side, *remote, put, narrow, back_first, mask, grad_two)
        total = mine.astype(F32) + swapped(mine, axis, bit).astype(F32)
        if step == 5:
            total, grad_features = lax.optimization_barrier((total, grad_features))
    scale = 1.0 / math.sqrt(SLOTS * lax.axis_size("tx") * lax.axis_size("ty") * EDGE**3)
    total = total * scale
    other = swapped(total, "ty", 1)
    return (result, grad_features, jnp.where(late, other, total), jnp.where(late, total, other))


def solution(mesh):
    return jax.shard_map(
        body,
        mesh=mesh,
        in_specs=(
            P(("tx", "ty"), None, None),
            P(("tx", "ty"), None),
            P(("tx", "ty"), None),
            P(),
            P(),
            P(("tx", "ty"), None, None),
        ),
        out_specs=(P(("tx", "ty"), None, None), P(("tx", "ty"), None, None), P(), P()),
        check_vma=False,
    )
```

```python
import math

import jax
import jax.numpy as jnp
from jax import lax
from jax.experimental import pallas as pl
from jax.experimental.pallas import tpu as pltpu
from jax.sharding import PartitionSpec as P


EDGE = 8
LANES = 128
PITCH = 10
SLOTS = 6
CHANS = 32
INNER = EDGE * LANES
WHOLE = (EDGE + 2) * LANES
BF16 = jnp.bfloat16
F32 = jnp.float32
VMEM_LIMIT = 16 * 1024 * 1024


def iota(dims, axis):
    return lax.broadcasted_iota(jnp.int32, dims, axis)


def one_hot(test):
    return jnp.where(test, 1.0, 0.0).astype(BF16)


def spread_lane(at):
    return (at >> 6) * LANES + ((at >> 3) % EDGE + 1) * PITCH + at % EDGE + 1


def widening():
    return one_hot(iota((LANES, 2 * LANES), 1) == spread_lane(iota((LANES, 1), 0)))


def narrowing():
    return one_hot(iota((2 * LANES, LANES), 0) == spread_lane(iota((1, LANES), 1)))


def face_lane(at, lanes):
    spot = at % EDGE
    group = at >> 6
    low_y, high_y, low_z, high_z = lanes
    lane = jnp.where(group == 0, low_y + spot, high_y + spot)
    lane = jnp.where(group == 2, (spot + 1) * PITCH + low_z, lane)
    lane = jnp.where(group == 3, (spot + 1) * PITCH + high_z, lane)
    return ((at >> 3) % EDGE) * LANES + lane


def picking():
    target = face_lane(iota((1, 256), 1), (EDGE * PITCH + 1, PITCH + 1, EDGE, 1))
    return one_hot(iota((INNER, 256), 0) == target)


def putting():
    target = face_lane(iota((256, 1), 0), (1, (EDGE + 1) * PITCH + 1, 0, EDGE + 1))
    return one_hot(iota((256, INNER), 1) == target)


def dot(lhs, rhs):
    return jnp.dot(lhs, rhs, preferred_element_type=F32)


def spread(field, matrix):
    return [dot(field[:, at * LANES : (at + 1) * LANES], matrix) for at in range(4)]


def emit_faces(place_ref, inner_ref, pick_ref, even_ref, odd_ref, side_ref, end_ref):
    raised = place_ref[1] == 1
    low = inner_ref[:, :, :LANES]
    high = inner_ref[:, :, INNER - LANES :]
    even_ref[...] = jnp.where(raised, low, high)
    odd_ref[...] = jnp.where(raised, high, low)
    flat = inner_ref[...].reshape(SLOTS * CHANS, INNER)
    found = dot(flat, pick_ref[...]).astype(BF16)
    side_ref[...] = found[:, :LANES].reshape(FACE)
    end_ref[...] = found[:, LANES:].reshape(FACE)


def build_cells(cells_ref, sheet_ref, inner_ref, side_ref, end_ref, remote_refs, put_ref, neighbours_ref, place_ref):
    base = place_ref[0]
    lane = lax.broadcasted_iota(jnp.int32, (1, LANES), 1)
    lower = (lane < 64).astype(F32).astype(BF16)
    upper = (lane >= 64).astype(F32).astype(BF16)
    zero = jnp.zeros((CHANS, LANES), BF16)

    x_odd_ref, x_even_ref, y_odd_ref, y_even_ref = remote_refs
    pairs = ((x_odd_ref, x_even_ref), (x_even_ref, x_odd_ref), (y_odd_ref, y_even_ref), (y_even_ref, y_odd_ref))

    def picked(slot, face, local):
        ident = neighbours_ref[slot, face]
        place = lax.rem(jnp.maximum(ident, 0), SLOTS)
        value = local(place)
        if face < 4:
            here = (ident >= base) & (ident < base + SLOTS)
            settled, raised = pairs[face]
            distant = jnp.where(place_ref[1 + face // 2] == 1, raised[place], settled[place])
            value = jnp.where(here, value, distant)
        return jnp.where(ident >= 0, value, zero)

    for slot in range(SLOTS):
        cells_ref[slot, :, :LANES] = picked(
            slot, 0, lambda at: inner_ref[at, :, INNER - LANES :]
        )
        cells_ref[slot, :, WHOLE - LANES :] = picked(
            slot, 1, lambda at: inner_ref[at, :, :LANES]
        )
        sides = lambda at: side_ref[at]
        ends = lambda at: end_ref[at]
        rows = pl.ds(slot * CHANS, CHANS)
        sheet_ref[rows, :LANES] = (
            picked(slot, 2, sides) * lower + picked(slot, 3, sides) * upper
        )
        sheet_ref[rows, LANES:] = (
            picked(slot, 4, ends) * lower + picked(slot, 5, ends) * upper
        )
    halo = dot(sheet_ref[...], put_ref[...]).astype(BF16).reshape(SLOTS, CHANS, INNER)
    cells_ref[:, :, LANES : LANES + INNER] = inner_ref[...] + halo


def shift_planes(columns_ref, cells_ref, slot):
    for plane in range(EDGE + 2):
        span = slice(plane * LANES, (plane + 1) * LANES)
        tile = cells_ref[slot, :, span]
        for tap in range(3):
            moved_tile = tile if tap == 1 else pltpu.roll(tile, (1 - tap) % LANES, 1)
            columns_ref[tap * CHANS : (tap + 1) * CHANS, span] = moved_tile


def windows(columns_ref):
    return jnp.concatenate([columns_ref[:, at * LANES : at * LANES + INNER] for at in range(3)], axis=0)


def stacked(weight):
    rows = []
    for mid in range(3):
        parts = [weight[:, (first * 3 + mid) * 96 : (first * 3 + mid + 1) * 96] for first in range(3)]
        rows.append(jnp.concatenate(parts, axis=1))
    return jnp.concatenate(rows, axis=0)


def turn_lanes(value, amount):
    return jnp.concatenate(
        [pltpu.roll(value[:, at * LANES : (at + 1) * LANES], amount % LANES, 1) for at in range(EDGE)], axis=1
    )


def convolve(columns_ref, weight):
    raw = dot(weight, windows(columns_ref))
    return (
        raw[CHANS : 2 * CHANS]
        + turn_lanes(raw[:CHANS], PITCH)
        + turn_lanes(raw[2 * CHANS :], -PITCH)
    )


def enter_kernel(place_ref, features_hbm, occupancy_hbm, inner_ref, mask_ref, pick_ref, even_ref, odd_ref, side_ref, end_ref,
                 features_ref, occupancy_ref, sems):
    loads = [
        pltpu.make_async_copy(occupancy_hbm, occupancy_ref, sems.at[0]),
        pltpu.make_async_copy(features_hbm, features_ref, sems.at[1]),
    ]
    for load in loads:
        load.start()
    pick_ref[...] = picking()
    matrix = widening()
    for load in loads:
        load.wait()
    mask = occupancy_ref[...].astype(F32).astype(BF16)
    for at, part in enumerate(spread(mask, matrix)):
        mask_ref[:, at * 256 : (at + 1) * 256] = part
    masked = jnp.concatenate(
        [features_ref[slot] * mask[slot : slot + 1, :] for slot in range(SLOTS)], axis=0
    )
    for at, part in enumerate(spread(masked, matrix)):
        inner_ref[:, :, at * 256 : (at + 1) * 256] = part.astype(BF16).reshape(SLOTS, CHANS, 256)
    emit_faces(place_ref, inner_ref, pick_ref, even_ref, odd_ref, side_ref, end_ref)


def turned(weight):
    taps = weight.astype(F32).T.astype(BF16)
    rows = []
    for mid in range(3):
        blocks = []
        for first in range(3):
            for last in range(3):
                tap = 26 - (first * 3 + mid) * 3 - last
                blocks.append(taps[tap * CHANS : (tap + 1) * CHANS])
        rows.append(jnp.concatenate(blocks, axis=1))
    return jnp.concatenate(rows, axis=0)


def prepare_kernel(cotangent_ref, mask_ref, first_ref, second_ref, out_ref, back_first_ref, back_second_ref, put_ref):
    put_ref[...] = putting()
    back_first_ref[...] = turned(first_ref[...])
    back_second_ref[...] = turned(second_ref[...])
    flat = cotangent_ref[...].reshape(SLOTS * CHANS, 512)
    for at, part in enumerate(spread(flat, widening())):
        span = slice(at * 256, (at + 1) * 256)
        for slot in range(SLOTS):
            out_ref[slot, :, span] = (
                part[slot * CHANS : (slot + 1) * CHANS] * mask_ref[slot : slot + 1, span]
            ).astype(BF16)


def first_kernel(neighbours_ref, place_ref, inner_ref, side_ref, end_ref, r0, r1, r2, r3, put_ref, pick_ref, weight_ref, mask_ref,
                 cells_ref, hidden_ref, even_ref, odd_ref, side_out_ref, end_out_ref, sheet_ref, columns_ref):
    build_cells(cells_ref, sheet_ref, inner_ref, side_ref, end_ref, (r0, r1, r2, r3), put_ref, neighbours_ref, place_ref)
    weight = stacked(weight_ref[...])
    for slot in range(SLOTS):
        buffer = columns_ref.at[slot % 2]
        shift_planes(buffer, cells_ref, slot)
        pre = convolve(buffer, weight)
        hidden_ref[slot] = (jnp.maximum(pre, 0.0) * mask_ref[slot : slot + 1, :]).astype(BF16)
    emit_faces(place_ref, hidden_ref, pick_ref, even_ref, odd_ref, side_out_ref, end_out_ref)


def pack_rows(inner, gather):
    return [dot(inner[:, at * 256 : (at + 1) * 256], gather) for at in range(4)]


def second_kernel(neighbours_ref, place_ref, inner_ref, side_ref, end_ref, r0, r1, r2, r3, put_ref, pick_ref, weight_ref,
                  mask_ref, skip_ref, cotangent_ref,
                  cells_ref, wide_ref, grad_ref, even_ref, odd_ref, side_out_ref, end_out_ref, sheet_ref, columns_ref):
    build_cells(cells_ref, sheet_ref, inner_ref, side_ref, end_ref, (r0, r1, r2, r3), put_ref, neighbours_ref, place_ref)
    weight = stacked(weight_ref[...])
    for slot in range(SLOTS):
        buffer = columns_ref.at[slot % 2]
        shift_planes(buffer, cells_ref, slot)
        pre = convolve(buffer, weight) + skip_ref[slot].astype(F32)
        wide_ref[slot] = (jnp.maximum(pre, 0.0) * mask_ref[slot : slot + 1, :]).astype(BF16)
        grad_ref[slot] = jnp.where(pre > 0.0, cotangent_ref[slot].astype(F32), 0.0).astype(BF16)
    emit_faces(place_ref, grad_ref, pick_ref, even_ref, odd_ref, side_out_ref, end_out_ref)


def pack_kernel(wide_ref, out_ref):
    flat = wide_ref[...].reshape(SLOTS * CHANS, INNER)
    for at, part in enumerate(pack_rows(flat, narrowing())):
        out_ref[:, :, at * LANES : (at + 1) * LANES] = part.astype(BF16).reshape(SLOTS, CHANS, LANES)


def third_kernel(neighbours_ref, place_ref, inner_ref, side_ref, end_ref, r0, r1, r2, r3, put_ref, pick_ref, weight_ref, mask_ref,
                 hidden_ref, grad_ref, even_ref, odd_ref, side_out_ref, end_out_ref, cells_ref, sheet_ref, columns_ref):
    build_cells(cells_ref, sheet_ref, inner_ref, side_ref, end_ref, (r0, r1, r2, r3), put_ref, neighbours_ref, place_ref)
    weight = weight_ref[...]
    for slot in range(SLOTS):
        buffer = columns_ref.at[slot % 2]
        shift_planes(buffer, cells_ref, slot)
        grad = convolve(buffer, weight) * mask_ref[slot : slot + 1, :]
        grad_ref[slot] = jnp.where(hidden_ref[slot].astype(F32) > 0.0, grad, 0.0).astype(BF16)
    emit_faces(place_ref, grad_ref, pick_ref, even_ref, odd_ref, side_out_ref, end_out_ref)


def last_kernel(neighbours_ref, place_ref, inner_ref, side_ref, end_ref, r0, r1, r2, r3, put_ref, weight_ref, mask_ref,
                grad_ref, out_ref, cells_ref, sheet_ref, columns_ref, wide_ref):
    build_cells(cells_ref, sheet_ref, inner_ref, side_ref, end_ref, (r0, r1, r2, r3), put_ref, neighbours_ref, place_ref)
    weight = weight_ref[...]
    for slot in range(SLOTS):
        buffer = columns_ref.at[slot % 2]
        shift_planes(buffer, cells_ref, slot)
        grad = convolve(buffer, weight) + grad_ref[slot].astype(F32)
        wide_ref[slot] = (grad * mask_ref[slot : slot + 1, :]).astype(BF16)
    flat = wide_ref[...].reshape(SLOTS * CHANS, INNER)
    for at, part in enumerate(pack_rows(flat, narrowing())):
        out_ref[:, :, at * LANES : (at + 1) * LANES] = part.astype(BF16).reshape(SLOTS, CHANS, LANES)


def weight_kernel(cells_ref, grad_ref, out_ref, columns_ref):
    total = jnp.zeros((9 * CHANS, 3 * CHANS), F32)
    for slot in range(SLOTS):
        buffer = columns_ref.at[slot % 2]
        shift_planes(buffer, cells_ref, slot)
        grad = grad_ref[slot]
        grads = jnp.concatenate([turn_lanes(grad, -PITCH), grad, turn_lanes(grad, PITCH)], axis=0)
        total = total + lax.dot_general(
            windows(buffer), grads, (((1,), (1,)), ((), ())), preferred_element_type=F32
        )
    flat = total.T
    for mid in range(3):
        for first in range(3):
            start = (first * 3 + mid) * 96
            out_ref[:, start : start + 96] = flat[mid * CHANS : (mid + 1) * CHANS, first * 96 : (first + 1) * 96]


def shape(dims, dtype=BF16):
    return jax.ShapeDtypeStruct(dims, dtype)


FIELD = (SLOTS, CHANS, 512)
INSIDE = (SLOTS, CHANS, INNER)
CELLS = (SLOTS, CHANS, WHOLE)
FACE = (SLOTS, CHANS, LANES)
FACES = [shape(FACE)] * 4
SCRATCH = [pltpu.VMEM((SLOTS * CHANS, 256), BF16), pltpu.VMEM((2, 3 * CHANS, WHOLE), BF16)]


def call(kernel, outs, scratch, scalars, flops, space=pltpu.VMEM):
    def run(*args):
        far = [at >= scalars and space == pltpu.HBM for at, a in enumerate(args)]
        args = [pltpu.with_memory_space_constraint(a, pltpu.HBM) if f else a for f, a in zip(far, args)]
        specs = [
            pl.BlockSpec(memory_space=pltpu.SMEM if at < scalars else pltpu.HBM if far[at] else pltpu.VMEM)
            for at in range(len(args))
        ]
        moved = sum(a.size * a.dtype.itemsize for a in args)
        moved += sum(math.prod(o.shape) * o.dtype.itemsize for o in outs)
        result = pl.pallas_call(
            kernel,
            out_shape=outs,
            in_specs=specs,
            out_specs=[pl.BlockSpec(memory_space=pltpu.VMEM)] * len(outs),
            scratch_shapes=scratch,
            compiler_params=pltpu.CompilerParams(vmem_limit_bytes=VMEM_LIMIT),
            cost_estimate=pl.CostEstimate(flops=flops, bytes_accessed=moved, transcendentals=0),
        )(*args)
        return result

    return run


AXES = ("tx", "ty")
RING_X, RING_Y, RING_Z = 4, 4, 8


def moved(value, to):
    pairs = []
    for source in range(RING_X * RING_Y * RING_Z * 2):
        row, col = divmod(source, RING_Z * 4)
        x, y_high = divmod(row, 2)
        y_low, rest = divmod(col, RING_Z * 2)
        z, core = divmod(rest, 2)
        x, y, z, core = to(x, y_high * 2 + y_low, z, core)
        x, y = x % RING_X, y % RING_Y
        pairs.append((source, ((x * 2 + y // 2) * 2 + y % 2) * RING_Z * 2 + z * 2 + core))
    return lax.ppermute(value, AXES, pairs)


def paired(value, axis, odd):
    count = lax.axis_size(axis)
    return lax.ppermute(
        value, axis, [(at, (at ^ 1) if not odd else (at + 1 if at % 2 else at - 1) % count) for at in range(count)]
    )


def other_core(value):
    return moved(value, lambda x, y, z, core: (x, y, z, core ^ 1))


ROUNDS = (
    (lambda x, y, z, c: (x, y, z ^ 3, c), lambda x, y, z, c: (x, y, z ^ 2, c), lambda x, y, z, c: (x, y, z ^ 1, c)),
    (lambda x, y, z, c: (x, y, z ^ 4, c),),
    (lambda x, y, z, c: (x, y + 2, z, c), lambda x, y, z, c: (x, y + 1, z, c), lambda x, y, z, c: (x, y - 1, z, c)),
    (lambda x, y, z, c: (x + 2, y, z, c), lambda x, y, z, c: (x + 1, y, z, c), lambda x, y, z, c: (x - 1, y, z, c)),
)
HOPS = (("tx", 1, "x_odd"), ("tx", 0, "x_even"), ("ty", 1, "y_odd"), ("ty", 0, "y_even"))


def hop(value, at):
    axis, odd, _ = HOPS[at]
    return paired(value, axis, odd)


def exchanged(odd, even, side):
    sent = (odd, even, side, side)
    return [hop(value, at) for at, value in enumerate(sent)]


CONV_FLOPS = 2 * 96 * 288 * WHOLE * SLOTS


RIDERS = ((), (0, 1, 2, 3), (), ())


def body(features, occupancy, neighbours, w_first, w_second, cotangent):
    row, col = lax.axis_index("tx"), lax.axis_index("ty")
    base = (row * lax.axis_size("ty") + col) * SLOTS
    place = jnp.stack([base, row % 2, col % 2]).astype(jnp.int32)
    place, late = lax.optimization_barrier((place, col % 2 == 1))
    enter_scratch = [
        pltpu.VMEM(FIELD, BF16),
        pltpu.VMEM((SLOTS, 512), jnp.int32),
        pltpu.SemaphoreType.DMA((2,)),
    ]
    x_inner, mask, pick, even, odd, side, end = call(
        enter_kernel,
        [shape(INSIDE), shape((SLOTS, INNER), F32), shape((INNER, 256))] + FACES,
        enter_scratch,
        1,
        2 * 192 * 512 * 1024,
        pltpu.HBM,
    )(place, features, occupancy)
    remote = exchanged(odd, even, side)
    cot_inner, back_first, back_second, put = call(
        prepare_kernel,
        [shape(INSIDE)] + [shape((3 * CHANS, 9 * CHANS))] * 2 + [shape((256, INNER))],
        [],
        0,
        2 * 192 * 512 * 256,
    )(cotangent, mask, w_first, w_second)
    x_cells, hidden, even, odd, hidden_side, hidden_end = call(
        first_kernel, [shape(CELLS), shape(INSIDE)] + FACES, SCRATCH, 2, CONV_FLOPS
    )(neighbours, place, x_inner, side, end, *remote, put, pick, w_first, mask)
    remote = exchanged(odd, even, hidden_side)
    hidden_cells, wide, grad_two, even, odd, grad_side, grad_end = call(
        second_kernel, [shape(CELLS), shape(INSIDE), shape(INSIDE)] + FACES, SCRATCH, 2, CONV_FLOPS
    )(neighbours, place, hidden, hidden_side, hidden_end, *remote, put, pick, w_second, mask, x_inner, cot_inner)
    remote = exchanged(odd, even, grad_side)
    weight_scratch = [SCRATCH[1]]
    weight_call = call(weight_kernel, [shape((CHANS, 27 * CHANS), F32)], weight_scratch, 0, CONV_FLOPS)
    (result,) = call(pack_kernel, [shape(FIELD)], [], 0, 2 * 192 * 1024 * 128)(wide)
    (term_second,) = weight_call(hidden_cells, grad_two)
    grad_one, even, odd, one_side, one_end = call(
        third_kernel, [shape(INSIDE)] + FACES, [pltpu.VMEM(CELLS, BF16)] + SCRATCH, 2, CONV_FLOPS
    )(neighbours, place, grad_two, grad_side, grad_end, *remote, put, pick, back_second, mask, hidden)
    (term_first,) = weight_call(x_cells, grad_one)
    sent = [odd, even, one_side, one_side]
    total = jnp.where(late, term_second, term_first) + other_core(jnp.where(late, term_first, term_second))
    remote = []
    for step, group in enumerate(ROUNDS):
        mine = total.astype(BF16)
        if step == len(ROUNDS) - 1:
            mine, remote = lax.optimization_barrier((mine, remote))
            (grad_features,) = call(
                last_kernel,
                [shape(FIELD)],
                [pltpu.VMEM(CELLS, BF16)] + SCRATCH + [pltpu.VMEM(INSIDE, BF16)],
                2,
                CONV_FLOPS,
            )(neighbours, place, grad_one, one_side, one_end, *remote, put, back_first, mask, grad_two)
        elif remote:
            mine, remote, result = lax.optimization_barrier((mine, remote, result))
        for at in RIDERS[step]:
            mine, value = lax.optimization_barrier((mine, sent[at]))
            remote.append(hop(value, at))
        parts = [mine.astype(F32)]
        for to in group:
            parts.append(moved(mine, to).astype(F32))
        total = parts[0] + parts[1]
        if len(parts) == 4:
            total = total + (parts[2] + parts[3])
        if step == len(ROUNDS) - 1:
            total, grad_features = lax.optimization_barrier((total, grad_features))
    scale = 1.0 / math.sqrt(SLOTS * lax.axis_size("tx") * lax.axis_size("ty") * EDGE**3)
    total = total * scale
    other = other_core(total)
    return (result, grad_features, jnp.where(late, other, total), jnp.where(late, total, other))


def solution(mesh):
    return jax.shard_map(
        body,
        mesh=mesh,
        in_specs=(
            P(("tx", "ty"), None, None),
            P(("tx", "ty"), None),
            P(("tx", "ty"), None),
            P(),
            P(),
            P(("tx", "ty"), None, None),
        ),
        out_specs=(P(("tx", "ty"), None, None), P(("tx", "ty"), None, None), P(), P()),
        check_vma=False,
    )
```

```python
import math

import jax
import jax.numpy as jnp
from jax import lax
from jax.experimental import pallas as pl
from jax.experimental.pallas import tpu as pltpu
from jax.sharding import PartitionSpec as P


EDGE = 8
LANES = 128
PITCH = 10
SLOTS = 6
CHANS = 32
INNER = EDGE * LANES
WHOLE = (EDGE + 2) * LANES
BF16 = jnp.bfloat16
F32 = jnp.float32
VMEM_LIMIT = 16 * 1024 * 1024


def iota(dims, axis):
    return lax.broadcasted_iota(jnp.int32, dims, axis)


def one_hot(test):
    return jnp.where(test, 1.0, 0.0).astype(BF16)


def spread_lane(at):
    return (at >> 6) * LANES + ((at >> 3) % EDGE + 1) * PITCH + at % EDGE + 1


def widening():
    return one_hot(iota((LANES, 2 * LANES), 1) == spread_lane(iota((LANES, 1), 0)))


def narrowing():
    return one_hot(iota((2 * LANES, LANES), 0) == spread_lane(iota((1, LANES), 1)))


def face_lane(at, lanes):
    spot = at % EDGE
    group = at >> 6
    low_y, high_y, low_z, high_z = lanes
    lane = jnp.where(group == 0, low_y + spot, high_y + spot)
    lane = jnp.where(group == 2, (spot + 1) * PITCH + low_z, lane)
    lane = jnp.where(group == 3, (spot + 1) * PITCH + high_z, lane)
    return ((at >> 3) % EDGE) * LANES + lane


def picking():
    target = face_lane(iota((1, 256), 1), (EDGE * PITCH + 1, PITCH + 1, EDGE, 1))
    return one_hot(iota((INNER, 256), 0) == target)


def putting():
    target = face_lane(iota((256, 1), 0), (1, (EDGE + 1) * PITCH + 1, 0, EDGE + 1))
    return one_hot(iota((256, INNER), 1) == target)


def dot(lhs, rhs):
    return jnp.dot(lhs, rhs, preferred_element_type=F32)


def spread(field, matrix):
    return [dot(field[:, at * LANES : (at + 1) * LANES], matrix) for at in range(4)]


def emit_faces(place_ref, inner_ref, pick_ref, even_ref, odd_ref, side_ref, end_ref):
    raised = place_ref[1] == 1
    low = inner_ref[:, :, :LANES]
    high = inner_ref[:, :, INNER - LANES :]
    even_ref[...] = jnp.where(raised, low, high)
    odd_ref[...] = jnp.where(raised, high, low)
    flat = inner_ref[...].reshape(SLOTS * CHANS, INNER)
    found = dot(flat, pick_ref[...]).astype(BF16)
    side_ref[...] = found[:, :LANES].reshape(FACE)
    end_ref[...] = found[:, LANES:].reshape(FACE)


def build_cells(cells_ref, sheet_ref, inner_ref, side_ref, end_ref, remote_refs, put_ref, neighbours_ref, place_ref):
    base = place_ref[0]
    lane = lax.broadcasted_iota(jnp.int32, (1, LANES), 1)
    lower = (lane < 64).astype(F32).astype(BF16)
    upper = (lane >= 64).astype(F32).astype(BF16)
    zero = jnp.zeros((CHANS, LANES), BF16)

    x_odd_ref, x_even_ref, y_odd_ref, y_even_ref = remote_refs
    pairs = ((x_odd_ref, x_even_ref), (x_even_ref, x_odd_ref), (y_odd_ref, y_even_ref), (y_even_ref, y_odd_ref))

    def picked(slot, face, local):
        ident = neighbours_ref[slot, face]
        place = lax.rem(jnp.maximum(ident, 0), SLOTS)
        value = local(place)
        if face < 4:
            here = (ident >= base) & (ident < base + SLOTS)
            settled, raised = pairs[face]
            distant = jnp.where(place_ref[1 + face // 2] == 1, raised[place], settled[place])
            value = jnp.where(here, value, distant)
        return jnp.where(ident >= 0, value, zero)

    for slot in range(SLOTS):
        cells_ref[slot, :, :LANES] = picked(
            slot, 0, lambda at: inner_ref[at, :, INNER - LANES :]
        )
        cells_ref[slot, :, WHOLE - LANES :] = picked(
            slot, 1, lambda at: inner_ref[at, :, :LANES]
        )
        sides = lambda at: side_ref[at]
        ends = lambda at: end_ref[at]
        rows = pl.ds(slot * CHANS, CHANS)
        sheet_ref[rows, :LANES] = (
            picked(slot, 2, sides) * lower + picked(slot, 3, sides) * upper
        )
        sheet_ref[rows, LANES:] = (
            picked(slot, 4, ends) * lower + picked(slot, 5, ends) * upper
        )
    halo = dot(sheet_ref[...], put_ref[...]).astype(BF16).reshape(SLOTS, CHANS, INNER)
    cells_ref[:, :, LANES : LANES + INNER] = inner_ref[...] + halo


def shift_planes(columns_ref, cells_ref, slot):
    for plane in range(EDGE + 2):
        span = slice(plane * LANES, (plane + 1) * LANES)
        tile = cells_ref[slot, :, span]
        for tap in range(3):
            moved_tile = tile if tap == 1 else pltpu.roll(tile, (1 - tap) % LANES, 1)
            columns_ref[tap * CHANS : (tap + 1) * CHANS, span] = moved_tile


def windows(columns_ref):
    return jnp.concatenate([columns_ref[:, at * LANES : at * LANES + INNER] for at in range(3)], axis=0)


def stacked(weight):
    rows = []
    for mid in range(3):
        parts = [weight[:, (first * 3 + mid) * 96 : (first * 3 + mid + 1) * 96] for first in range(3)]
        rows.append(jnp.concatenate(parts, axis=1))
    return jnp.concatenate(rows, axis=0)


def turn_lanes(value, amount):
    return jnp.concatenate(
        [pltpu.roll(value[:, at * LANES : (at + 1) * LANES], amount % LANES, 1) for at in range(EDGE)], axis=1
    )


def convolve(columns_ref, weight):
    raw = dot(weight, windows(columns_ref))
    return (
        raw[CHANS : 2 * CHANS]
        + turn_lanes(raw[:CHANS], PITCH)
        + turn_lanes(raw[2 * CHANS :], -PITCH)
    )


def enter_kernel(place_ref, features_hbm, occupancy_hbm, inner_ref, mask_ref, pick_ref, even_ref, odd_ref, side_ref, end_ref,
                 features_ref, occupancy_ref, sems):
    loads = [
        pltpu.make_async_copy(occupancy_hbm, occupancy_ref, sems.at[0]),
        pltpu.make_async_copy(features_hbm, features_ref, sems.at[1]),
    ]
    for load in loads:
        load.start()
    pick_ref[...] = picking()
    matrix = widening()
    for load in loads:
        load.wait()
    mask = occupancy_ref[...].astype(F32).astype(BF16)
    for at, part in enumerate(spread(mask, matrix)):
        mask_ref[:, at * 256 : (at + 1) * 256] = part
    masked = jnp.concatenate(
        [features_ref[slot] * mask[slot : slot + 1, :] for slot in range(SLOTS)], axis=0
    )
    for at, part in enumerate(spread(masked, matrix)):
        inner_ref[:, :, at * 256 : (at + 1) * 256] = part.astype(BF16).reshape(SLOTS, CHANS, 256)
    emit_faces(place_ref, inner_ref, pick_ref, even_ref, odd_ref, side_ref, end_ref)


def turned(weight):
    taps = weight.astype(F32).T.astype(BF16)
    rows = []
    for mid in range(3):
        blocks = []
        for first in range(3):
            for last in range(3):
                tap = 26 - (first * 3 + mid) * 3 - last
                blocks.append(taps[tap * CHANS : (tap + 1) * CHANS])
        rows.append(jnp.concatenate(blocks, axis=1))
    return jnp.concatenate(rows, axis=0)


def prepare_kernel(cotangent_ref, mask_ref, first_ref, second_ref, out_ref, back_first_ref, back_second_ref, put_ref):
    put_ref[...] = putting()
    back_first_ref[...] = turned(first_ref[...])
    back_second_ref[...] = turned(second_ref[...])
    flat = cotangent_ref[...].reshape(SLOTS * CHANS, 512)
    for at, part in enumerate(spread(flat, widening())):
        span = slice(at * 256, (at + 1) * 256)
        for slot in range(SLOTS):
            out_ref[slot, :, span] = (
                part[slot * CHANS : (slot + 1) * CHANS] * mask_ref[slot : slot + 1, span]
            ).astype(BF16)


def first_kernel(neighbours_ref, place_ref, inner_ref, side_ref, end_ref, r0, r1, r2, r3, put_ref, pick_ref, weight_ref, mask_ref,
                 cells_ref, hidden_ref, even_ref, odd_ref, side_out_ref, end_out_ref, sheet_ref, columns_ref):
    build_cells(cells_ref, sheet_ref, inner_ref, side_ref, end_ref, (r0, r1, r2, r3), put_ref, neighbours_ref, place_ref)
    weight = stacked(weight_ref[...])
    for slot in range(SLOTS):
        buffer = columns_ref.at[slot % 2]
        shift_planes(buffer, cells_ref, slot)
        pre = convolve(buffer, weight)
        hidden_ref[slot] = (jnp.maximum(pre, 0.0) * mask_ref[slot : slot + 1, :]).astype(BF16)
    emit_faces(place_ref, hidden_ref, pick_ref, even_ref, odd_ref, side_out_ref, end_out_ref)


def pack_rows(inner, gather):
    return [dot(inner[:, at * 256 : (at + 1) * 256], gather) for at in range(4)]


def second_kernel(neighbours_ref, place_ref, inner_ref, side_ref, end_ref, r0, r1, r2, r3, put_ref, pick_ref, weight_ref,
                  mask_ref, skip_ref, cotangent_ref,
                  cells_ref, wide_ref, grad_ref, even_ref, odd_ref, side_out_ref, end_out_ref, sheet_ref, columns_ref):
    build_cells(cells_ref, sheet_ref, inner_ref, side_ref, end_ref, (r0, r1, r2, r3), put_ref, neighbours_ref, place_ref)
    weight = stacked(weight_ref[...])
    for slot in range(SLOTS):
        buffer = columns_ref.at[slot % 2]
        shift_planes(buffer, cells_ref, slot)
        pre = convolve(buffer, weight) + skip_ref[slot].astype(F32)
        wide_ref[slot] = (jnp.maximum(pre, 0.0) * mask_ref[slot : slot + 1, :]).astype(BF16)
        grad_ref[slot] = jnp.where(pre > 0.0, cotangent_ref[slot].astype(F32), 0.0).astype(BF16)
    emit_faces(place_ref, grad_ref, pick_ref, even_ref, odd_ref, side_out_ref, end_out_ref)


def pack_kernel(wide_ref, out_ref):
    flat = wide_ref[...].reshape(SLOTS * CHANS, INNER)
    for at, part in enumerate(pack_rows(flat, narrowing())):
        out_ref[:, :, at * LANES : (at + 1) * LANES] = part.astype(BF16).reshape(SLOTS, CHANS, LANES)


def third_kernel(neighbours_ref, place_ref, inner_ref, side_ref, end_ref, r0, r1, r2, r3, put_ref, pick_ref, weight_ref, mask_ref,
                 hidden_ref, grad_ref, even_ref, odd_ref, side_out_ref, end_out_ref, cells_ref, sheet_ref, columns_ref):
    build_cells(cells_ref, sheet_ref, inner_ref, side_ref, end_ref, (r0, r1, r2, r3), put_ref, neighbours_ref, place_ref)
    weight = weight_ref[...]
    for slot in range(SLOTS):
        buffer = columns_ref.at[slot % 2]
        shift_planes(buffer, cells_ref, slot)
        grad = convolve(buffer, weight) * mask_ref[slot : slot + 1, :]
        grad_ref[slot] = jnp.where(hidden_ref[slot].astype(F32) > 0.0, grad, 0.0).astype(BF16)
    emit_faces(place_ref, grad_ref, pick_ref, even_ref, odd_ref, side_out_ref, end_out_ref)


def last_kernel(neighbours_ref, place_ref, inner_ref, side_ref, end_ref, r0, r1, r2, r3, put_ref, weight_ref, mask_ref,
                grad_ref, out_ref, cells_ref, sheet_ref, columns_ref, wide_ref):
    build_cells(cells_ref, sheet_ref, inner_ref, side_ref, end_ref, (r0, r1, r2, r3), put_ref, neighbours_ref, place_ref)
    weight = weight_ref[...]
    for slot in range(SLOTS):
        buffer = columns_ref.at[slot % 2]
        shift_planes(buffer, cells_ref, slot)
        grad = convolve(buffer, weight) + grad_ref[slot].astype(F32)
        wide_ref[slot] = (grad * mask_ref[slot : slot + 1, :]).astype(BF16)
    flat = wide_ref[...].reshape(SLOTS * CHANS, INNER)
    for at, part in enumerate(pack_rows(flat, narrowing())):
        out_ref[:, :, at * LANES : (at + 1) * LANES] = part.astype(BF16).reshape(SLOTS, CHANS, LANES)


def weight_kernel(cells_ref, grad_ref, out_ref, columns_ref):
    total = jnp.zeros((9 * CHANS, 3 * CHANS), F32)
    for slot in range(SLOTS):
        buffer = columns_ref.at[slot % 2]
        shift_planes(buffer, cells_ref, slot)
        grad = grad_ref[slot]
        grads = jnp.concatenate([turn_lanes(grad, -PITCH), grad, turn_lanes(grad, PITCH)], axis=0)
        total = total + lax.dot_general(
            windows(buffer), grads, (((1,), (1,)), ((), ())), preferred_element_type=F32
        )
    flat = total.T
    for mid in range(3):
        for first in range(3):
            start = (first * 3 + mid) * 96
            out_ref[:, start : start + 96] = flat[mid * CHANS : (mid + 1) * CHANS, first * 96 : (first + 1) * 96]


def shape(dims, dtype=BF16):
    return jax.ShapeDtypeStruct(dims, dtype)


FIELD = (SLOTS, CHANS, 512)
INSIDE = (SLOTS, CHANS, INNER)
CELLS = (SLOTS, CHANS, WHOLE)
FACE = (SLOTS, CHANS, LANES)
FACES = [shape(FACE)] * 4
SCRATCH = [pltpu.VMEM((SLOTS * CHANS, 256), BF16), pltpu.VMEM((2, 3 * CHANS, WHOLE), BF16)]


def call(kernel, outs, scratch, scalars, flops, space=pltpu.VMEM):
    def run(*args):
        far = [at >= scalars and space == pltpu.HBM for at, a in enumerate(args)]
        args = [pltpu.with_memory_space_constraint(a, pltpu.HBM) if f else a for f, a in zip(far, args)]
        specs = [
            pl.BlockSpec(memory_space=pltpu.SMEM if at < scalars else pltpu.HBM if far[at] else pltpu.VMEM)
            for at in range(len(args))
        ]
        moved = sum(a.size * a.dtype.itemsize for a in args)
        moved += sum(math.prod(o.shape) * o.dtype.itemsize for o in outs)
        result = pl.pallas_call(
            kernel,
            out_shape=outs,
            in_specs=specs,
            out_specs=[pl.BlockSpec(memory_space=pltpu.VMEM)] * len(outs),
            scratch_shapes=scratch,
            compiler_params=pltpu.CompilerParams(vmem_limit_bytes=VMEM_LIMIT),
            cost_estimate=pl.CostEstimate(flops=flops, bytes_accessed=moved, transcendentals=0),
        )(*args)
        return result

    return run


AXES = ("tx", "ty")
RING_X, RING_Y, RING_Z = 4, 4, 8


def moved(value, to):
    pairs = []
    for source in range(RING_X * RING_Y * RING_Z * 2):
        row, col = divmod(source, RING_Z * 4)
        x, y_high = divmod(row, 2)
        y_low, rest = divmod(col, RING_Z * 2)
        z, core = divmod(rest, 2)
        x, y, z, core = to(x, y_high * 2 + y_low, z, core)
        x, y = x % RING_X, y % RING_Y
        pairs.append((source, ((x * 2 + y // 2) * 2 + y % 2) * RING_Z * 2 + z * 2 + core))
    return lax.ppermute(value, AXES, pairs)


def paired(value, axis, odd):
    count = lax.axis_size(axis)
    return lax.ppermute(
        value, axis, [(at, (at ^ 1) if not odd else (at + 1 if at % 2 else at - 1) % count) for at in range(count)]
    )


def other_core(value):
    return moved(value, lambda x, y, z, core: (x, y, z, core ^ 1))


ROUNDS = (
    (lambda x, y, z, c: (x, y, z ^ 1, c), lambda x, y, z, c: (x, y, z ^ 2, c), lambda x, y, z, c: (x, y, z ^ 3, c)),
    (lambda x, y, z, c: (x, y, z ^ 4, c),),
    (lambda x, y, z, c: (x, y + 2, z, c), lambda x, y, z, c: (x, y + 1, z, c), lambda x, y, z, c: (x, y - 1, z, c)),
    (lambda x, y, z, c: (x + 2, y, z, c), lambda x, y, z, c: (x + 1, y, z, c), lambda x, y, z, c: (x - 1, y, z, c)),
)
HOPS = (("tx", 1, "x_odd"), ("tx", 0, "x_even"), ("ty", 1, "y_odd"), ("ty", 0, "y_even"))


def hop(value, at):
    axis, odd, _ = HOPS[at]
    return paired(value, axis, odd)


def exchanged(odd, even, side):
    sent = (odd, even, side, side)
    return [hop(value, at) for at, value in enumerate(sent)]


CONV_FLOPS = 2 * 96 * 288 * WHOLE * SLOTS


RIDERS = ((), (0, 1, 2, 3), (), ())


def body(features, occupancy, neighbours, w_first, w_second, cotangent):
    row, col = lax.axis_index("tx"), lax.axis_index("ty")
    base = (row * lax.axis_size("ty") + col) * SLOTS
    place = jnp.stack([base, row % 2, col % 2]).astype(jnp.int32)
    place, late = lax.optimization_barrier((place, col % 2 == 1))
    enter_scratch = [
        pltpu.VMEM(FIELD, BF16),
        pltpu.VMEM((SLOTS, 512), jnp.int32),
        pltpu.SemaphoreType.DMA((2,)),
    ]
    x_inner, mask, pick, even, odd, side, end = call(
        enter_kernel,
        [shape(INSIDE), shape((SLOTS, INNER), F32), shape((INNER, 256))] + FACES,
        enter_scratch,
        1,
        2 * 192 * 512 * 1024,
        pltpu.HBM,
    )(place, features, occupancy)
    remote = exchanged(odd, even, side)
    cot_inner, back_first, back_second, put = call(
        prepare_kernel,
        [shape(INSIDE)] + [shape((3 * CHANS, 9 * CHANS))] * 2 + [shape((256, INNER))],
        [],
        0,
        2 * 192 * 512 * 256,
    )(cotangent, mask, w_first, w_second)
    x_cells, hidden, even, odd, hidden_side, hidden_end = call(
        first_kernel, [shape(CELLS), shape(INSIDE)] + FACES, SCRATCH, 2, CONV_FLOPS
    )(neighbours, place, x_inner, side, end, *remote, put, pick, w_first, mask)
    remote = exchanged(odd, even, hidden_side)
    hidden_cells, wide, grad_two, even, odd, grad_side, grad_end = call(
        second_kernel, [shape(CELLS), shape(INSIDE), shape(INSIDE)] + FACES, SCRATCH, 2, CONV_FLOPS
    )(neighbours, place, hidden, hidden_side, hidden_end, *remote, put, pick, w_second, mask, x_inner, cot_inner)
    remote = exchanged(odd, even, grad_side)
    weight_scratch = [SCRATCH[1]]
    weight_call = call(weight_kernel, [shape((CHANS, 27 * CHANS), F32)], weight_scratch, 0, CONV_FLOPS)
    (term_second,) = weight_call(hidden_cells, grad_two)
    grad_one, even, odd, one_side, one_end = call(
        third_kernel, [shape(INSIDE)] + FACES, [pltpu.VMEM(CELLS, BF16)] + SCRATCH, 2, CONV_FLOPS
    )(neighbours, place, grad_two, grad_side, grad_end, *remote, put, pick, back_second, mask, hidden)
    (term_first,) = weight_call(x_cells, grad_one)
    sent = [odd, even, one_side, one_side]
    given = jnp.where(late, term_first, term_second).astype(BF16)
    total = jnp.where(late, term_second, term_first) + other_core(given).astype(F32)
    remote = []
    for step, group in enumerate(ROUNDS):
        mine = total.astype(BF16)
        if step == 2:
            mine, wide = lax.optimization_barrier((mine, wide))
            (result,) = call(pack_kernel, [shape(FIELD)], [], 0, 2 * 192 * 1024 * 128)(wide)
        if step == len(ROUNDS) - 1:
            mine, remote, result = lax.optimization_barrier((mine, remote, result))
            (grad_features,) = call(
                last_kernel,
                [shape(FIELD)],
                [pltpu.VMEM(CELLS, BF16)] + SCRATCH + [pltpu.VMEM(INSIDE, BF16)],
                2,
                CONV_FLOPS,
            )(neighbours, place, grad_one, one_side, one_end, *remote, put, back_first, mask, grad_two)
        elif remote:
            mine, remote = lax.optimization_barrier((mine, remote))
        for at in RIDERS[step]:
            mine, value = lax.optimization_barrier((mine, sent[at]))
            remote.append(hop(value, at))
        parts = [mine.astype(F32)]
        for to in group:
            parts.append(moved(mine, to).astype(F32))
        total = parts[0] + parts[1]
        if len(parts) == 4:
            total = total + (parts[2] + parts[3])
        if step == len(ROUNDS) - 1:
            total, grad_features = lax.optimization_barrier((total, grad_features))
    scale = 1.0 / math.sqrt(SLOTS * lax.axis_size("tx") * lax.axis_size("ty") * EDGE**3)
    total = total * scale
    other = other_core(total)
    return (result, grad_features, jnp.where(late, other, total), jnp.where(late, total, other))


def solution(mesh):
    return jax.shard_map(
        body,
        mesh=mesh,
        in_specs=(
            P(("tx", "ty"), None, None),
            P(("tx", "ty"), None),
            P(("tx", "ty"), None),
            P(),
            P(),
            P(("tx", "ty"), None, None),
        ),
        out_specs=(P(("tx", "ty"), None, None), P(("tx", "ty"), None, None), P(), P()),
        check_vma=False,
    )
```
